32 devices in a mesh: dp: 8 (over z, x), expert: 4 (over y, core).
Axes of the slice: x: 2, y: 2, z: 4, core: 2. Of those that a mesh axis runs over, the one named last changes fastest.
Arguments:
- tokens: bfloat16 [8192, 1024], P(('dp', 'expert')), may hold values from -6 to 6
- expert_ids: int32 [8192, 2], P(('dp', 'expert')), may hold values from 0 to 31, all different within a row; in each aligned block of 256 rows (0 to 255, 256 to 511, ...) at most 40 rows name the same one
- gate_quant: int32 [8192], P(('dp', 'expert')), may hold values from 1 to 255
- cotangent: bfloat16 [8192, 1024], P(('dp', 'expert')), may hold values from -3 to 3
- w_gate: bfloat16 [32, 1024, 512], P('expert'), may hold values from -0.1875 to 0.1875
- w_up: bfloat16 [32, 1024, 512], P('expert'), may hold values from -0.1875 to 0.1875
- w_down: bfloat16 [32, 512, 1024], P('expert'), may hold values from -0.25 to 0.25
Outputs:
- layer_out: bfloat16 [8192, 1024], P(('dp', 'expert'))
- grad_tokens: bfloat16 [8192, 1024], P(('dp', 'expert'))
- grad_w_gate: float32 [32, 1024, 512], P('expert', 'dp')
- grad_w_up: float32 [32, 1024, 512], P('expert', 'dp')
- grad_w_down: float32 [32, 512, 1024], P('expert', 'dp')
The draws below stay inside these ranges and needn't reach their ends.
Inputs may be any that keep to these rules, and one draw needn't show every extreme that they name: `expert_ids`: each row names two different experts. Within the 256 rows of one device no expert is named more than 40 times, and in every draw some device names some expert exactly 40 times.
All inputs are finite; a program needn't handle non-finite values.
Results may differ from the reference program's by a relative error of at most 0.017.
Values may be sent and summed in bfloat16 or wider, within the bound.
A program may use at most 128 MiB of HBM per device.

```python
import math
import jax
import jax.numpy as jnp
import numpy as np
from jax import lax

D = 1024
HID = 512
EXPERTS = 32
TOK_DEV = 256
CAP = 40
TOKENS = 8192
N_DP = 8
N_EXPERT = 4


def with_ends(drawn, key, least, top_value):
    index_at = [jax.random.randint(jax.random.fold_in(key, axis), (), 0, length) for axis, length in enumerate(drawn.shape)]
    widest = drawn.shape.index(max(drawn.shape))
    beside = index_at[:widest] + [(index_at[widest] + 1) % drawn.shape[widest]] + index_at[widest + 1:]
    return drawn.at[tuple(index_at)].set(least).at[tuple(beside)].set(top_value)


def raised(array, key, source, target, shards_of, factor):
    def block_of(dim):
        return (jnp.arange(array.shape[dim]) // (array.shape[dim] // shards_of)).reshape((-1,) + (1,) * (array.ndim - 1 - dim))

    one_side = jax.random.permutation(key, shards_of)[block_of(target)]
    far = (block_of(target) + shards_of // 2) % shards_of
    return jnp.where((block_of(source) == one_side) | (block_of(source) == far), factor * array, array)


def steps_of(own_key, shape, cuts, smallest, high):
    def one(axis_at, shards_of):
        heights = jax.random.uniform(jax.random.fold_in(jax.random.fold_in(own_key, 6), axis_at), (shards_of,), jnp.float32, smallest / len(cuts), high / len(cuts))
        return jnp.repeat(jnp.exp(heights), shape[axis_at] // shards_of).reshape((-1,) + (1,) * (len(shape) - axis_at - 1))

    level = one(*cuts[0])
    for cut in cuts[1:]:
        level = level * one(*cut)
    return level


def routed_block(own_key, own, number, rows, count, top, bound, lean):
    sequence = jax.random.permutation(own_key, count)
    crowded, usual = portions_of(count, rows * top, bound, lean, True), portions_of(count, rows * top, bound, lean, False)
    places = jnp.arange(count)

    def named(tallies, turn):
        used = int((tallies > 0).sum())
        fixed = max(1, used // 4)
        moved = fixed + (places - fixed + turn * (used - fixed)) % max(1, count - fixed)
        return jnp.zeros((count,), jnp.int32).at[sequence[jnp.where(places < fixed, places, moved)]].set(jnp.asarray(tallies, jnp.int32))

    tallies = jnp.where(number % 4 == 0, named(crowded, number // 4), named(usual, number - number // 4 - 1))
    mixed = jax.random.permutation(jax.random.fold_in(own, 3), count)
    giver, taker = mixed[0:count // 2 * 2:2], mixed[1:count // 2 * 2:2]
    room = jnp.minimum(tallies[giver] - 1, bound - tallies[taker]) // 2
    room = jnp.where((giver == sequence[0]) | (taker == sequence[0]) | (tallies[taker] == 0), 0, jnp.maximum(room, 0))
    moved = jax.random.randint(jax.random.fold_in(own, 4), (count // 2,), 0, 1 << 20) % (room + 1)
    tallies = tallies.at[giver].add(-moved).at[taker].add(moved)
    labels = jnp.searchsorted(jnp.cumsum(tallies), jnp.arange(rows * top), side="right").astype(jnp.int32)
    table = labels.reshape(top, rows).T
    table = table[jax.random.permutation(jax.random.fold_in(own, 1), rows)]
    turn = jax.random.randint(jax.random.fold_in(own, 2), (rows, 1), 0, top)
    return jnp.take_along_axis(table, (jnp.arange(top)[None, :] + turn) % top, axis=1)


def portions_of(count, total, limit, lean, full):
    weights = [(1 << 20) // math.isqrt(standing ** lean) + 1 for standing in range(1, count + 1)]
    largest = limit if full else min(limit, max(-(-total // count), total * weights[0] // sum(weights)))
    least = 1 if total - largest >= count - 1 else 0
    holding, spare = [largest] + [least] * (count - 1), total - largest - least * (count - 1)
    while spare > 0:
        free = [i for i in range(1, count) if holding[i] < largest] or [i for i in range(1, count) if holding[i] < limit]
        whole, remaining = sum([weights[i] for i in free]), spare
        for i in free:
            addition = min(limit - holding[i], max(1, remaining * weights[i] // whole), spare)
            holding[i] = holding[i] + addition
            spare = spare - addition
    return np.array(holding)


def scatter_about(own_key, dims, width, bound, split=(), held_as=jnp.bfloat16):
    values = jax.random.normal(own_key, dims, jnp.float32) * width
    if len(split) > 0:
        values = steps_of(own_key, dims, split, -0.22, 0.18) * values
    return jnp.clip(values, min=-bound, max=bound).astype(held_as)


def noise_with(rng, dims, spread, limit, pieces, heavy, held_as=jnp.bfloat16):
    array = spread * jax.random.normal(rng, dims, jnp.float32)
    if pieces:
        array = array * steps_of(rng, dims, pieces, -0.22, 0.18)
    return jnp.clip(raised(array, jax.random.fold_in(rng, 3), *heavy), -limit, limit).astype(held_as)


def setup_inputs(seed: int = 0) -> dict:
    key_of = jax.random.split(jax.random.key(seed), 8)
    tokens = noise_with(key_of[0], (TOKENS, D), 1.0, 6.0, ((0, 32),), (0, 1, 32, 2.75))
    expert_ids_keys = jax.random.split(jax.random.fold_in(key_of[1], 1), TOKENS // TOK_DEV)
    expert_ids_turns = jax.random.permutation(jax.random.fold_in(key_of[1], 3), TOKENS // TOK_DEV)
    expert_ids = jax.vmap(lambda own, number: routed_block(jax.random.fold_in(key_of[1], 2), own, number, TOK_DEV, EXPERTS, 2, CAP, 2))(expert_ids_keys, expert_ids_turns).reshape((TOKENS, 2))
    gate_quant = with_ends(jax.random.randint(key_of[2], (TOKENS,), 1, 256), jax.random.fold_in(key_of[2], 1), 1, 255).astype(jnp.int32)
    cotangent = scatter_about(key_of[3], (TOKENS, D), 0.5, 3.0, ((0, 32),))
    w_gate = scatter_about(key_of[4], (EXPERTS, D, HID), D ** -0.5, 0.1875, ((0, 4),))
    w_up = scatter_about(key_of[5], (EXPERTS, D, HID), D ** -0.5, 0.1875, ((0, 4),))
    w_down = scatter_about(key_of[6], (EXPERTS, HID, D), HID ** -0.5, 0.25, ((0, 4),))
    return dict(tokens=tokens, expert_ids=expert_ids, gate_quant=gate_quant, cotangent=cotangent, w_gate=w_gate, w_up=w_up, w_down=w_down)


def slot_places(expert_ids):
    flat_ids = expert_ids.reshape(-1)
    choose = (flat_ids[:, None] == jnp.arange(EXPERTS, dtype=jnp.int32)[None, :]).astype(jnp.int32)
    earlier = jnp.cumsum(choose, axis=0) - choose
    return (flat_ids * CAP + jnp.sum(earlier * choose, axis=1)).astype(jnp.int32)


def place_rows(slot_index, values):
    blank_rows = jnp.zeros((EXPERTS * CAP, values.shape[1]), values.dtype)
    return blank_rows.at[slot_index].set(values)


def by_expert(sent):
    return sent.reshape(N_EXPERT, EXPERTS, CAP, D).transpose(1, 0, 2, 3).reshape(EXPERTS, N_EXPERT * CAP, D)


def from_expert(result):
    return result.reshape(EXPERTS, N_EXPERT, CAP, D).transpose(1, 0, 2, 3).reshape(N_EXPERT, EXPERTS * CAP, D)


def expert_pass(operands):
    token_rows, routed_rows, gate_weight, up_weight, down_weight = operands
    gate_value = jnp.dot(token_rows, gate_weight, preferred_element_type=jnp.float32)
    up_value = jnp.dot(token_rows, up_weight, preferred_element_type=jnp.float32)
    sigmoid_gate = jax.nn.sigmoid(gate_value)
    activated = gate_value * sigmoid_gate
    hidden = (activated * up_value).astype(jnp.bfloat16)
    expert_out = jnp.dot(hidden, down_weight, preferred_element_type=jnp.float32).astype(jnp.bfloat16)
    hidden_grad = jnp.dot(routed_rows, down_weight.T, preferred_element_type=jnp.float32)
    gate_grad = (hidden_grad * up_value * sigmoid_gate * (1.0 + gate_value * (1.0 - sigmoid_gate))).astype(jnp.bfloat16)
    up_grad = (hidden_grad * activated).astype(jnp.bfloat16)
    input_grad = (jnp.dot(gate_grad, gate_weight.T, preferred_element_type=jnp.float32)
                  + jnp.dot(up_grad, up_weight.T, preferred_element_type=jnp.float32)).astype(jnp.bfloat16)
    part_gate = jnp.dot(token_rows.T, gate_grad, preferred_element_type=jnp.float32).astype(jnp.bfloat16)
    part_up = jnp.dot(token_rows.T, up_grad, preferred_element_type=jnp.float32).astype(jnp.bfloat16)
    part_down = jnp.dot(hidden.T, routed_rows, preferred_element_type=jnp.float32).astype(jnp.bfloat16)
    return expert_out, input_grad, part_gate, part_up, part_down


def pick_rows(rows_back, places):
    return rows_back[places]


def reference(tokens, expert_ids, gate_quant, cotangent, w_gate, w_up, w_down):
    def group_pass(totals, group_data):
        group_tokens, group_ids, group_quant, group_cot = group_data
        slot_index = jax.vmap(slot_places)(group_ids)
        first_share = group_quant.astype(jnp.float32) / 256.0
        shares = jnp.stack([first_share, 1.0 - first_share], axis=2)
        doubled = jnp.repeat(group_tokens, 2, axis=1)
        routed = (shares[:, :, :, None] * group_cot[:, :, None, :].astype(jnp.float32)).astype(jnp.bfloat16)
        routed = routed.reshape(N_EXPERT, 2 * TOK_DEV, D)
        sent_tokens = jax.vmap(place_rows)(slot_index, doubled)
        sent_grads = jax.vmap(place_rows)(slot_index, routed)
        expert_out, input_grad, part_gate, part_up, part_down = lax.map(
            expert_pass, (by_expert(sent_tokens), by_expert(sent_grads), w_gate, w_up, w_down))
        picked = jax.vmap(pick_rows)(from_expert(expert_out), slot_index)
        picked = picked.reshape(N_EXPERT, TOK_DEV, 2, D).astype(jnp.float32)
        layer_out = jnp.sum(shares[:, :, :, None] * picked, axis=2).astype(jnp.bfloat16)
        picked_grad = jax.vmap(pick_rows)(from_expert(input_grad), slot_index)
        picked_grad = picked_grad.reshape(N_EXPERT, TOK_DEV, 2, D).astype(jnp.float32)
        grad_tokens = (picked_grad[:, :, 0] + picked_grad[:, :, 1]).astype(jnp.bfloat16)
        totals = (totals[0] + part_gate.astype(jnp.float32),
                  totals[1] + part_up.astype(jnp.float32),
                  totals[2] + part_down.astype(jnp.float32))
        return totals, (layer_out, grad_tokens)

    initial = (jnp.zeros((EXPERTS, D, HID), jnp.float32),
               jnp.zeros((EXPERTS, D, HID), jnp.float32),
               jnp.zeros((EXPERTS, HID, D), jnp.float32))
    inputs = (tokens.reshape(N_DP, N_EXPERT, TOK_DEV, D),
              expert_ids.reshape(N_DP, N_EXPERT, TOK_DEV, 2),
              gate_quant.reshape(N_DP, N_EXPERT, TOK_DEV),
              cotangent.reshape(N_DP, N_EXPERT, TOK_DEV, D))
    totals, stacked = lax.scan(group_pass, initial, inputs)
    layer_out = stacked[0].reshape(TOKENS, D)
    grad_tokens = stacked[1].reshape(TOKENS, D)
    return (layer_out, grad_tokens, totals[0], totals[1], totals[2])
```

```python
import jax
import jax.numpy as jnp
from jax import lax
from jax.sharding import PartitionSpec as P

CAP = 40


def slot_places(expert_ids, experts):
    flat_ids = expert_ids.reshape(-1)
    choose = (flat_ids[:, None] == jnp.arange(experts, dtype=jnp.int32)[None, :]).astype(jnp.int32)
    earlier = jnp.cumsum(choose, axis=0) - choose
    return flat_ids * CAP + jnp.sum(earlier * choose, axis=1)


def expert_forward(received, w_gate, w_up, w_down):
    gate_value = jnp.einsum(
        "aserd,edh->aserh", received, w_gate, preferred_element_type=jnp.float32
    )
    up_value = jnp.einsum("aserd,edh->aserh", received, w_up, preferred_element_type=jnp.float32)
    sigmoid_gate = jax.nn.sigmoid(gate_value)
    hidden = (gate_value * sigmoid_gate * up_value).astype(jnp.bfloat16)
    expert_out = jnp.einsum(
        "aserh,ehd->aserd", hidden, w_down, preferred_element_type=jnp.float32
    ).astype(jnp.bfloat16)
    return (gate_value, up_value, hidden, expert_out)


def expert_backward(routed, gate_value, up_value, w_gate, w_up, w_down):
    hidden_grad = jnp.einsum("aserd,ehd->aserh", routed, w_down, preferred_element_type=jnp.float32)
    sigmoid_gate = jax.nn.sigmoid(gate_value)
    gate_grad = (
        hidden_grad * up_value * sigmoid_gate * (1.0 + gate_value * (1.0 - sigmoid_gate))
    ).astype(jnp.bfloat16)
    up_grad = (hidden_grad * (gate_value * sigmoid_gate)).astype(jnp.bfloat16)
    input_grad = (
        jnp.einsum("aserh,edh->aserd", gate_grad, w_gate, preferred_element_type=jnp.float32)
        + jnp.einsum("aserh,edh->aserd", up_grad, w_up, preferred_element_type=jnp.float32)
    ).astype(jnp.bfloat16)
    return (gate_grad, up_grad, input_grad)


def to_owner(rows):
    n_dp = lax.axis_size("dp")
    _, s, e, r, d = rows.shape
    by_expert = rows[0].transpose(1, 0, 2, 3)
    got = lax.all_to_all(by_expert, "dp", split_axis=0, concat_axis=0, tiled=True)
    own = e // n_dp
    return got.reshape(n_dp, own, s, r, d).transpose(1, 0, 2, 3, 4).reshape(own, n_dp * s * r, d)


def owner_grads(token_rows, routed_rows, w_gate, w_up, w_down):
    gate_value = jnp.einsum("ord,odh->orh", token_rows, w_gate, preferred_element_type=jnp.float32)
    up_value = jnp.einsum("ord,odh->orh", token_rows, w_up, preferred_element_type=jnp.float32)
    hidden_grad = jnp.einsum(
        "ord,ohd->orh", routed_rows, w_down, preferred_element_type=jnp.float32
    )
    s = jax.nn.sigmoid(gate_value)
    activated = gate_value * s
    hidden = (activated * up_value).astype(jnp.bfloat16)
    gate_grad = (hidden_grad * up_value * s * (1.0 + gate_value * (1.0 - s))).astype(jnp.bfloat16)
    up_grad = (hidden_grad * activated).astype(jnp.bfloat16)
    total_gate = jnp.einsum(
        "ord,orh->odh", token_rows, gate_grad, preferred_element_type=jnp.float32
    )
    total_up = jnp.einsum("ord,orh->odh", token_rows, up_grad, preferred_element_type=jnp.float32)
    total_down = jnp.einsum(
        "orh,ord->ohd", hidden, routed_rows, preferred_element_type=jnp.float32
    )
    return total_gate, total_up, total_down


def to_shards(total):
    n_dp = lax.axis_size("dp")
    own, rows, cols = total.shape
    cut = total.astype(jnp.bfloat16).reshape(own, n_dp, rows // n_dp, cols).transpose(1, 0, 2, 3)
    got = lax.all_to_all(cut, "dp", split_axis=0, concat_axis=0, tiled=True)
    return got.reshape(n_dp * own, rows // n_dp, cols).astype(jnp.float32)


def summed_shards(left, right, rows):
    term = jnp.einsum(rows, left, right, preferred_element_type=jnp.float32).astype(jnp.bfloat16)
    return lax.psum_scatter(term, "dp", scatter_dimension=1, tiled=True).astype(jnp.float32)


def per_device(tokens, expert_ids, gate_quant, cotangent, w_gate, w_up, w_down):
    groups = lax.axis_size("expert")
    n_dp = lax.axis_size("dp")
    local_experts, d, _ = w_gate.shape
    experts = groups * local_experts
    slot_index = slot_places(expert_ids, experts)
    first_share = gate_quant.astype(jnp.float32) / 256.0
    shares = jnp.stack([first_share, 1.0 - first_share], axis=1)
    doubled = jnp.repeat(tokens, 2, axis=0)
    routed_rows = (
        (shares[:, :, None] * cotangent[:, None, :].astype(jnp.float32))
        .astype(jnp.bfloat16)
        .reshape(-1, d)
    )
    blank_rows = jnp.zeros((experts * CAP, d), jnp.bfloat16)
    layout = (groups, 1, local_experts, CAP, d)
    send_tokens = blank_rows.at[slot_index].set(doubled).reshape(layout)
    send_grads = blank_rows.at[slot_index].set(routed_rows).reshape(layout)
    received = lax.all_to_all(send_tokens, "expert", split_axis=0, concat_axis=1, tiled=True)
    routed = lax.all_to_all(send_grads, "expert", split_axis=0, concat_axis=1, tiled=True)
    gate_value, up_value, hidden, expert_out = expert_forward(received, w_gate, w_up, w_down)
    gate_grad, up_grad, input_grad = expert_backward(
        routed, gate_value, up_value, w_gate, w_up, w_down
    )
    if local_experts % n_dp == 0:
        own = local_experts // n_dp
        start = lax.axis_index("dp") * own
        mine = [lax.dynamic_slice_in_dim(w, start, own, axis=0) for w in (w_gate, w_up, w_down)]
        totals = owner_grads(to_owner(received), to_owner(routed), *mine)
        grad_w_gate, grad_w_up, grad_w_down = [to_shards(t) for t in totals]
    else:
        grad_w_gate = summed_shards(received, gate_grad, "aserd,aserh->edh")
        grad_w_up = summed_shards(received, up_grad, "aserd,aserh->edh")
        grad_w_down = summed_shards(hidden, routed, "aserh,aserd->ehd")
    returned = lax.all_to_all(expert_out, "expert", split_axis=1, concat_axis=0, tiled=True)
    returned_grad = lax.all_to_all(input_grad, "expert", split_axis=1, concat_axis=0, tiled=True)
    picked = returned.reshape(experts * CAP, d)[slot_index].reshape(-1, 2, d)
    layer_out = jnp.sum(shares[:, :, None] * picked.astype(jnp.float32), axis=1).astype(
        jnp.bfloat16
    )
    picked_grad = (
        returned_grad.reshape(experts * CAP, d)[slot_index].reshape(-1, 2, d).astype(jnp.float32)
    )
    grad_tokens = (picked_grad[:, 0] + picked_grad[:, 1]).astype(jnp.bfloat16)
    return (layer_out, grad_tokens, grad_w_gate, grad_w_up, grad_w_down)


def solution(mesh):
    return jax.shard_map(
        per_device,
        mesh=mesh,
        in_specs=(
            P(("dp", "expert"), None),
            P(("dp", "expert"), None),
            P(("dp", "expert")),
            P(("dp", "expert"), None),
            P("expert", None, None),
            P("expert", None, None),
            P("expert", None, None),
        ),
        out_specs=(
            P(("dp", "expert"), None),
            P(("dp", "expert"), None),
            P("expert", "dp", None),
            P("expert", "dp", None),
            P("expert", "dp", None),
        ),
        check_vma=False,
    )
```

```python
import jax
import jax.numpy as jnp
from jax import lax
from jax.sharding import PartitionSpec as P

CAP = 40


def slot_places(expert_ids, experts):
    flat_ids = expert_ids.reshape(-1)
    choose = (flat_ids[:, None] == jnp.arange(experts, dtype=jnp.int32)[None, :]).astype(jnp.int32)
    earlier = jnp.cumsum(choose, axis=0) - choose
    return flat_ids * CAP + jnp.sum(earlier * choose, axis=1)


def expert_forward(received, w_gate, w_up, w_down):
    gate_value = jnp.einsum(
        "aserd,edh->aserh", received, w_gate, preferred_element_type=jnp.float32
    )
    up_value = jnp.einsum("aserd,edh->aserh", received, w_up, preferred_element_type=jnp.float32)
    sigmoid_gate = jax.nn.sigmoid(gate_value)
    hidden = (gate_value * sigmoid_gate * up_value).astype(jnp.bfloat16)
    expert_out = jnp.einsum(
        "aserh,ehd->aserd", hidden, w_down, preferred_element_type=jnp.float32
    ).astype(jnp.bfloat16)
    return (gate_value, up_value, hidden, expert_out)


def expert_backward(routed, gate_value, up_value, w_gate, w_up, w_down):
    hidden_grad = jnp.einsum("aserd,ehd->aserh", routed, w_down, preferred_element_type=jnp.float32)
    sigmoid_gate = jax.nn.sigmoid(gate_value)
    gate_grad = (
        hidden_grad * up_value * sigmoid_gate * (1.0 + gate_value * (1.0 - sigmoid_gate))
    ).astype(jnp.bfloat16)
    up_grad = (hidden_grad * (gate_value * sigmoid_gate)).astype(jnp.bfloat16)
    input_grad = (
        jnp.einsum("aserh,edh->aserd", gate_grad, w_gate, preferred_element_type=jnp.float32)
        + jnp.einsum("aserh,edh->aserd", up_grad, w_up, preferred_element_type=jnp.float32)
    ).astype(jnp.bfloat16)
    return (gate_grad, up_grad, input_grad)


def exchanged(blocks):
    n_dp = lax.axis_size("dp")
    me = lax.axis_index("dp")
    got = [lax.dynamic_index_in_dim(blocks, me, 0, keepdims=False)]
    for step in range(1, n_dp):
        block = lax.dynamic_index_in_dim(blocks, lax.rem(me + step, n_dp), 0, keepdims=False)
        ring = [(i, (i + step) % n_dp) for i in range(n_dp)]
        got.append(lax.ppermute(block, "dp", ring))
    return got


def to_owner(rows):
    n_dp = lax.axis_size("dp")
    _, s, e, r, d = rows.shape
    own = e // n_dp
    by_expert = rows[0].transpose(1, 0, 2, 3).reshape(n_dp, own, s * r, d)
    return jnp.concatenate(exchanged(by_expert), axis=1)


def owner_grads(token_rows, routed_rows, w_gate, w_up, w_down):
    gate_value = jnp.einsum("ord,odh->orh", token_rows, w_gate, preferred_element_type=jnp.float32)
    up_value = jnp.einsum("ord,odh->orh", token_rows, w_up, preferred_element_type=jnp.float32)
    hidden_grad = jnp.einsum(
        "ord,ohd->orh", routed_rows, w_down, preferred_element_type=jnp.float32
    )
    s = jax.nn.sigmoid(gate_value)
    activated = gate_value * s
    hidden = (activated * up_value).astype(jnp.bfloat16)
    gate_grad = (hidden_grad * up_value * s * (1.0 + gate_value * (1.0 - s))).astype(jnp.bfloat16)
    up_grad = (hidden_grad * activated).astype(jnp.bfloat16)
    total_down = jnp.einsum(
        "orh,ord->ohd", hidden, routed_rows, preferred_element_type=jnp.float32
    )
    both_grads = jnp.concatenate([gate_grad, up_grad], axis=2)
    total_both = jnp.einsum(
        "ord,orh->odh", token_rows, both_grads, preferred_element_type=jnp.float32
    )
    return total_down, total_both


def to_shards(total):
    n_dp = lax.axis_size("dp")
    me = lax.axis_index("dp")
    own, rows, cols = total.shape
    cut = total.astype(jnp.bfloat16).reshape(own, n_dp, rows // n_dp, cols).transpose(1, 0, 2, 3)
    got = exchanged(cut)
    shards = jnp.zeros((n_dp, own, rows // n_dp, cols), jnp.float32)
    for step, block in enumerate(got):
        source = lax.rem(me - step + n_dp, n_dp)
        shards = lax.dynamic_update_index_in_dim(shards, block.astype(jnp.float32), source, 0)
    return shards.reshape(n_dp * own, rows // n_dp, cols)


def summed_shards(left, right, rows):
    term = jnp.einsum(rows, left, right, preferred_element_type=jnp.float32).astype(jnp.bfloat16)
    return lax.psum_scatter(term, "dp", scatter_dimension=1, tiled=True).astype(jnp.float32)


def per_device(tokens, expert_ids, gate_quant, cotangent, w_gate, w_up, w_down):
    groups = lax.axis_size("expert")
    n_dp = lax.axis_size("dp")
    local_experts, d, _ = w_gate.shape
    experts = groups * local_experts
    slot_index = slot_places(expert_ids, experts)
    first_share = gate_quant.astype(jnp.float32) / 256.0
    shares = jnp.stack([first_share, 1.0 - first_share], axis=1)
    doubled = jnp.repeat(tokens, 2, axis=0)
    routed_rows = (
        (shares[:, :, None] * cotangent[:, None, :].astype(jnp.float32))
        .astype(jnp.bfloat16)
        .reshape(-1, d)
    )
    blank_rows = jnp.zeros((experts * CAP, d), jnp.bfloat16)
    layout = (groups, 1, local_experts, CAP, d)
    send_tokens = blank_rows.at[slot_index].set(doubled).reshape(layout)
    send_grads = blank_rows.at[slot_index].set(routed_rows).reshape(layout)
    received = lax.all_to_all(send_tokens, "expert", split_axis=0, concat_axis=1, tiled=True)
    routed = lax.all_to_all(send_grads, "expert", split_axis=0, concat_axis=1, tiled=True)
    gate_value, up_value, hidden, expert_out = expert_forward(received, w_gate, w_up, w_down)
    gate_grad, up_grad, input_grad = expert_backward(
        routed, gate_value, up_value, w_gate, w_up, w_down
    )
    if local_experts % n_dp == 0:
        own = local_experts // n_dp
        start = lax.axis_index("dp") * own
        mine = [lax.dynamic_slice_in_dim(w, start, own, axis=0) for w in (w_gate, w_up, w_down)]
        totals = owner_grads(to_owner(received), to_owner(routed), *mine)
        grad_w_down, grad_both = [to_shards(t) for t in totals]
        grad_w_gate, grad_w_up = jnp.split(grad_both, 2, axis=2)
    else:
        grad_w_gate = summed_shards(received, gate_grad, "aserd,aserh->edh")
        grad_w_up = summed_shards(received, up_grad, "aserd,aserh->edh")
        grad_w_down = summed_shards(hidden, routed, "aserh,aserd->ehd")
    returned = lax.all_to_all(expert_out, "expert", split_axis=1, concat_axis=0, tiled=True)
    returned_grad = lax.all_to_all(input_grad, "expert", split_axis=1, concat_axis=0, tiled=True)
    picked = returned.reshape(experts * CAP, d)[slot_index].reshape(-1, 2, d)
    layer_out = jnp.sum(shares[:, :, None] * picked.astype(jnp.float32), axis=1).astype(
        jnp.bfloat16
    )
    picked_grad = (
        returned_grad.reshape(experts * CAP, d)[slot_index].reshape(-1, 2, d).astype(jnp.float32)
    )
    grad_tokens = (picked_grad[:, 0] + picked_grad[:, 1]).astype(jnp.bfloat16)
    return (layer_out, grad_tokens, grad_w_gate, grad_w_up, grad_w_down)


def solution(mesh):
    return jax.shard_map(
        per_device,
        mesh=mesh,
        in_specs=(
            P(("dp", "expert"), None),
            P(("dp", "expert"), None),
            P(("dp", "expert")),
            P(("dp", "expert"), None),
            P("expert", None, None),
            P("expert", None, None),
            P("expert", None, None),
        ),
        out_specs=(
            P(("dp", "expert"), None),
            P(("dp", "expert"), None),
            P("expert", "dp", None),
            P("expert", "dp", None),
            P("expert", "dp", None),
        ),
        check_vma=False,
    )
```

```python
import jax
import jax.numpy as jnp
from jax import lax
from jax.sharding import PartitionSpec as P

CAP = 40


def slot_places(expert_ids, experts):
    flat_ids = expert_ids.reshape(-1)
    choose = (flat_ids[:, None] == jnp.arange(experts, dtype=jnp.int32)[None, :]).astype(jnp.int32)
    earlier = jnp.cumsum(choose, axis=0) - choose
    return flat_ids * CAP + jnp.sum(earlier * choose, axis=1)


def expert_forward(received, w_gate, w_up, w_down):
    gate_value = jnp.einsum(
        "aserd,edh->aserh", received, w_gate, preferred_element_type=jnp.float32
    )
    up_value = jnp.einsum("aserd,edh->aserh", received, w_up, preferred_element_type=jnp.float32)
    sigmoid_gate = jax.nn.sigmoid(gate_value)
    hidden = (gate_value * sigmoid_gate * up_value).astype(jnp.bfloat16)
    expert_out = jnp.einsum(
        "aserh,ehd->aserd", hidden, w_down, preferred_element_type=jnp.float32
    ).astype(jnp.bfloat16)
    return (gate_value, up_value, hidden, expert_out)


def expert_backward(routed, gate_value, up_value, w_gate, w_up, w_down):
    hidden_grad = jnp.einsum("aserd,ehd->aserh", routed, w_down, preferred_element_type=jnp.float32)
    sigmoid_gate = jax.nn.sigmoid(gate_value)
    gate_grad = (
        hidden_grad * up_value * sigmoid_gate * (1.0 + gate_value * (1.0 - sigmoid_gate))
    ).astype(jnp.bfloat16)
    up_grad = (hidden_grad * (gate_value * sigmoid_gate)).astype(jnp.bfloat16)
    input_grad = (
        jnp.einsum("aserh,edh->aserd", gate_grad, w_gate, preferred_element_type=jnp.float32)
        + jnp.einsum("aserh,edh->aserd", up_grad, w_up, preferred_element_type=jnp.float32)
    ).astype(jnp.bfloat16)
    return (gate_grad, up_grad, input_grad)


def exchanged(blocks):
    n_dp = lax.axis_size("dp")
    me = lax.axis_index("dp")
    got = [lax.dynamic_index_in_dim(blocks, me, 0, keepdims=False)]
    for step in range(1, n_dp):
        block = lax.dynamic_index_in_dim(blocks, lax.rem(me + step, n_dp), 0, keepdims=False)
        ring = [(i, (i + step) % n_dp) for i in range(n_dp)]
        got.append(lax.ppermute(block, "dp", ring))
    return got


def to_owner(rows):
    n_dp = lax.axis_size("dp")
    _, s, e, r, d = rows.shape
    own = e // n_dp
    by_expert = rows[0].transpose(1, 0, 2, 3).reshape(n_dp, own, s * r, d)
    return jnp.concatenate(exchanged(by_expert), axis=1)


def owner_grads(token_rows, routed_rows, w_gate, w_up, w_down):
    gate_value = jnp.einsum("ord,odh->orh", token_rows, w_gate, preferred_element_type=jnp.float32)
    up_value = jnp.einsum("ord,odh->orh", token_rows, w_up, preferred_element_type=jnp.float32)
    hidden_grad = jnp.einsum(
        "ord,ohd->orh", routed_rows, w_down, preferred_element_type=jnp.float32
    )
    s = jax.nn.sigmoid(gate_value)
    activated = gate_value * s
    hidden = (activated * up_value).astype(jnp.bfloat16)
    gate_grad = (hidden_grad * up_value * s * (1.0 + gate_value * (1.0 - s))).astype(jnp.bfloat16)
    up_grad = (hidden_grad * activated).astype(jnp.bfloat16)
    total_down = jnp.einsum(
        "orh,ord->ohd", hidden, routed_rows, preferred_element_type=jnp.float32
    )
    both_grads = jnp.concatenate([gate_grad, up_grad], axis=2)
    total_both = jnp.einsum(
        "ord,orh->odh", token_rows, both_grads, preferred_element_type=jnp.float32
    )
    return total_down, total_both


def to_shards(total, parts):
    n_dp = lax.axis_size("dp")
    me = lax.axis_index("dp")
    own, rows, cols = total.shape
    cut = total.astype(jnp.bfloat16).reshape(own, n_dp, rows // n_dp, cols).transpose(1, 0, 2, 3)
    got = exchanged(cut)
    shards = [jnp.zeros((n_dp, own, rows // n_dp, cols // parts), jnp.float32)] * parts
    for step, block in enumerate(got):
        source = lax.rem(me - step + n_dp, n_dp)
        pieces = jnp.split(block.astype(jnp.float32), parts, axis=2)
        shards = [
            lax.dynamic_update_index_in_dim(shard, piece, source, 0)
            for shard, piece in zip(shards, pieces)
        ]
    return [shard.reshape(n_dp * own, rows // n_dp, cols // parts) for shard in shards]


def summed_shards(left, right, rows):
    term = jnp.einsum(rows, left, right, preferred_element_type=jnp.float32).astype(jnp.bfloat16)
    return lax.psum_scatter(term, "dp", scatter_dimension=1, tiled=True).astype(jnp.float32)


def per_device(tokens, expert_ids, gate_quant, cotangent, w_gate, w_up, w_down):
    groups = lax.axis_size("expert")
    n_dp = lax.axis_size("dp")
    local_experts, d, _ = w_gate.shape
    experts = groups * local_experts
    slot_index = slot_places(expert_ids, experts)
    first_share = gate_quant.astype(jnp.float32) / 256.0
    shares = jnp.stack([first_share, 1.0 - first_share], axis=1)
    doubled = jnp.repeat(tokens, 2, axis=0)
    routed_rows = (
        (shares[:, :, None] * cotangent[:, None, :].astype(jnp.float32))
        .astype(jnp.bfloat16)
        .reshape(-1, d)
    )
    blank_rows = jnp.zeros((experts * CAP, d), jnp.bfloat16)
    layout = (groups, 1, local_experts, CAP, d)
    send_tokens = blank_rows.at[slot_index].set(doubled).reshape(layout)
    send_grads = blank_rows.at[slot_index].set(routed_rows).reshape(layout)
    received = lax.all_to_all(send_tokens, "expert", split_axis=0, concat_axis=1, tiled=True)
    routed = lax.all_to_all(send_grads, "expert", split_axis=0, concat_axis=1, tiled=True)
    gate_value, up_value, hidden, expert_out = expert_forward(received, w_gate, w_up, w_down)
    gate_grad, up_grad, input_grad = expert_backward(
        routed, gate_value, up_value, w_gate, w_up, w_down
    )
    if local_experts % n_dp == 0:
        own = local_experts // n_dp
        start = lax.axis_index("dp") * own
        mine = [lax.dynamic_slice_in_dim(w, start, own, axis=0) for w in (w_gate, w_up, w_down)]
        own_tokens = to_owner(received)
        own_routed = to_owner(routed)
        totals = owner_grads(own_tokens, own_routed, *mine)
        grad_w_gate, grad_w_up = to_shards(totals[1], 2)
        (grad_w_down,) = to_shards(totals[0], 1)
    else:
        grad_w_gate = summed_shards(received, gate_grad, "aserd,aserh->edh")
        grad_w_up = summed_shards(received, up_grad, "aserd,aserh->edh")
        grad_w_down = summed_shards(hidden, routed, "aserh,aserd->ehd")
    returned = lax.all_to_all(expert_out, "expert", split_axis=1, concat_axis=0, tiled=True)
    returned_grad = lax.all_to_all(input_grad, "expert", split_axis=1, concat_axis=0, tiled=True)
    picked = returned.reshape(experts * CAP, d)[slot_index].reshape(-1, 2, d)
    layer_out = jnp.sum(shares[:, :, None] * picked.astype(jnp.float32), axis=1).astype(
        jnp.bfloat16
    )
    picked_grad = returned_grad.reshape(experts * CAP, d)[slot_index].reshape(-1, 2, d)
    picked_grad = picked_grad.astype(jnp.float32)
    grad_tokens = (picked_grad[:, 0] + picked_grad[:, 1]).astype(jnp.bfloat16)
    return (layer_out, grad_tokens, grad_w_gate, grad_w_up, grad_w_down)


def solution(mesh):
    return jax.shard_map(
        per_device,
        mesh=mesh,
        in_specs=(
            P(("dp", "expert"), None),
            P(("dp", "expert"), None),
            P(("dp", "expert")),
            P(("dp", "expert"), None),
            P("expert", None, None),
            P("expert", None, None),
            P("expert", None, None),
        ),
        out_specs=(
            P(("dp", "expert"), None),
            P(("dp", "expert"), None),
            P("expert", "dp", None),
            P("expert", "dp", None),
            P("expert", "dp", None),
        ),
        check_vma=False,
    )
```
